32 devices in a mesh: tok: 8 (over z, core), hid: 4 (over y, x).
Axes of the slice: x: 2, y: 2, z: 4, core: 2. Of those that a mesh axis runs over, the one named last changes fastest.
Arguments:
- tokens: bfloat16 [4096, 8192], P('tok', 'hid'), may hold values from -6 to 6
- sparse_weight: bfloat16 [128, 6, 256, 256], P('hid'), may hold values from -0.15625 to 0.15625
- low_left: bfloat16 [8192, 256], P('hid'), may hold values from -0.0625 to 0.0625
- low_right: bfloat16 [256, 32768], P(None, 'hid'), may hold values from -0.375 to 0.375
- act_grad: bfloat16 [4096, 32768], P('tok', 'hid'), may hold values from -6 to 6
Outputs:
- activated: bfloat16 [4096, 32768], P('tok', 'hid')
- tok_grad: bfloat16 [4096, 8192], P('tok', 'hid')
- weight_grad: bfloat16 [128, 6, 256, 256], P('hid', None, 'tok')
- left_grad: bfloat16 [8192, 256], P('hid', 'tok')
- right_grad: bfloat16 [256, 32768], P('tok', 'hid')
The draws below stay inside these ranges and needn't reach their ends.
All inputs are finite; a program needn't handle non-finite values.
Results may differ from the reference program's by a relative error of at most 0.02.
Values may be sent and summed in bfloat16 or wider, within the bound.
No kernel may reach another device: no remote copies, remote signals or barrier semaphores. Data moves between devices by JAX's collectives and lax.ppermute only.
A program may use at most 576 MiB of HBM per device.

```python
import jax
import jax.numpy as jnp
import numpy as np
from jax import lax

D = 8192
H = 32768
B = 256
R = 256
LOG_ROWS = 5
BITS = 2
SLOTS = 6
ROW_BLOCKS = 8
COL_BLOCKS = 128
TOKENS = 4096
N_HID = 4


def shard_levels(rng, dims, split, least, top_value):
    def one(position, shards_of):
        heights = jax.random.uniform(jax.random.fold_in(jax.random.fold_in(rng, 6), position), (shards_of,), jnp.float32, least / len(split), top_value / len(split))
        return jnp.repeat(jnp.exp(heights), dims[position] // shards_of).reshape((-1,) + (1,) * (len(dims) - position - 1))

    gain = one(*split[0])
    for cut in split[1:]:
        gain = gain * one(*cut)
    return gain


def centred(own_key, extent, width, reach, cuts=(), held_as=jnp.bfloat16):
    result = width * jax.random.normal(own_key, extent, jnp.float32)
    if cuts:
        result = result * shard_levels(own_key, extent, cuts, -0.22, 0.18)
    return jnp.clip(result, -reach, reach).astype(held_as)


def setup_inputs(seed: int = 0) -> dict:
    streams_of = jax.random.split(jax.random.key(seed), 6)
    return {
        "tokens": centred(streams_of[0], (TOKENS, D), 1.0, 6.0, ((0, 8), (1, 4))),
        "sparse_weight": centred(streams_of[1], (COL_BLOCKS, SLOTS, B, B), (SLOTS * B) ** -0.5, 0.15625, ((0, 4),)),
        "low_left": centred(streams_of[2], (D, R), D ** -0.5, 0.0625, ((0, 4),)),
        "low_right": centred(streams_of[3], (R, H), R ** -0.5, 0.375, ((1, 4),)),
        "act_grad": centred(streams_of[4], (TOKENS, H), 1.0, 6.0, ((0, 8), (1, 4))),
    }


def inner_rows(left, right):
    return lax.dot_general(left, right, (((0,), (0,)), ((), ())), preferred_element_type=jnp.float32)


def outer_cols(left, right):
    return lax.dot_general(left, right, (((1,), (1,)), ((), ())), preferred_element_type=jnp.float32)


def slot_table(cols_dev, row_blocks, local_bits, levels):
    home_rows = np.arange(cols_dev) // (cols_dev // row_blocks)
    flip_masks = [0] + [1 << bit_level for bit_level in range(local_bits)] + [0] * levels
    return np.stack([home_rows ^ flip_mask for flip_mask in flip_masks], axis=1).astype(np.int32)


def reference(tokens, sparse_weight, low_left, low_right, act_grad):
    tok_total = tokens.shape[0]
    cols_dev = H // (B * N_HID)
    hid_dev = H // N_HID
    local_bits = LOG_ROWS - BITS
    index_arr = jnp.asarray(slot_table(cols_dev, ROW_BLOCKS, local_bits, BITS), dtype=jnp.int32)
    selector = (index_arr[:, :, None] == jnp.arange(ROW_BLOCKS, dtype=jnp.int32)[None, None, :]).astype(jnp.float32)
    all_blocks = tokens.reshape(tok_total, D // B, B)
    low_rank = jnp.dot(tokens, low_left, preferred_element_type=jnp.float32).astype(jnp.bfloat16)

    def device_step(state_pair, device):
        row_sum, low_back = state_pair
        weight_dev = lax.dynamic_slice_in_dim(sparse_weight, device * cols_dev, cols_dev, 0)
        right_dev = lax.dynamic_slice_in_dim(low_right, device * hid_dev, hid_dev, 1)
        grad_dev = lax.dynamic_slice_in_dim(act_grad, device * hid_dev, hid_dev, 1)
        partners = [jnp.bitwise_xor(device, 1 << bit_level).astype(jnp.int32) for bit_level in range(BITS)]
        owner_arr = jnp.stack([device.astype(jnp.int32)] * (local_bits + 1) + partners).astype(jnp.int32)
        rows = (owner_arr[None, :] * ROW_BLOCKS + index_arr).astype(jnp.int32)
        picked = jnp.take(all_blocks, rows.reshape(-1), axis=1).reshape(tok_total, cols_dev, SLOTS, B).astype(jnp.float32)
        weight_f = weight_dev.astype(jnp.float32)
        sparse = jnp.einsum("tjkb,jkbc->tjc", picked, weight_f).reshape(tok_total, hid_dev)
        pre_act = sparse + jnp.dot(low_rank, right_dev, preferred_element_type=jnp.float32)
        gate_sig = jax.nn.sigmoid(pre_act)
        activated = (pre_act * gate_sig).astype(jnp.bfloat16)
        back_grad = (grad_dev.astype(jnp.float32) * gate_sig * (1.0 + pre_act * (1.0 - gate_sig))).astype(jnp.bfloat16)
        back_cols = back_grad.reshape(tok_total, cols_dev, B).astype(jnp.float32)
        contrib = jnp.einsum("tjc,jkbc->tjkb", back_cols, weight_f)
        routed = jnp.einsum("tjkb,jkr->ktrb", contrib, selector, precision=lax.Precision.HIGHEST)
        own_part = lax.optimization_barrier(jnp.sum(routed[:local_bits + 1], axis=0).astype(jnp.bfloat16))
        place_at = (device * ROW_BLOCKS).astype(jnp.int32)
        segment = lax.dynamic_slice_in_dim(row_sum, place_at, ROW_BLOCKS, 1) + own_part.astype(jnp.float32)
        row_sum = lax.dynamic_update_slice_in_dim(row_sum, segment, place_at, 1)
        for bit_level in range(BITS):
            sent_part = lax.optimization_barrier(routed[local_bits + 1 + bit_level].astype(jnp.bfloat16))
            place_at = (partners[bit_level] * ROW_BLOCKS).astype(jnp.int32)
            segment = lax.dynamic_slice_in_dim(row_sum, place_at, ROW_BLOCKS, 1) + sent_part.astype(jnp.float32)
            row_sum = lax.dynamic_update_slice_in_dim(row_sum, segment, place_at, 1)
        low_back = low_back + outer_cols(back_grad, right_dev)
        block_grad = jnp.einsum("tjkb,tjc->jkbc", picked, back_cols).astype(jnp.bfloat16)
        right_grad = inner_rows(low_rank, back_grad).astype(jnp.bfloat16)
        return (row_sum, low_back), (activated, block_grad, right_grad)

    start_pair = (jnp.zeros((tok_total, D // B, B), jnp.float32), jnp.zeros((tok_total, R), jnp.float32))
    final_pair, stacked = lax.scan(device_step, start_pair, jnp.arange(N_HID, dtype=jnp.int32))
    row_sum, low_back = final_pair
    act_stack, block_stack, right_stack = stacked
    activated = act_stack.transpose(1, 0, 2).reshape(tok_total, H)
    weight_grad = block_stack.reshape(COL_BLOCKS, SLOTS, B, B)
    right_grad = right_stack.transpose(1, 0, 2).reshape(R, H)
    low_back_b = low_back.astype(jnp.bfloat16)
    tok_grad = (row_sum.reshape(tok_total, D) + outer_cols(low_back_b, low_left)).astype(jnp.bfloat16)
    left_grad = inner_rows(tokens, low_back_b).astype(jnp.bfloat16)
    return (activated, tok_grad, weight_grad, left_grad, right_grad)
```

```python
import functools

import jax
import jax.numpy as jnp
from jax import lax
from jax.experimental import pallas as pl
from jax.experimental.pallas import tpu as pltpu
from jax.sharding import PartitionSpec as P


F32 = jnp.float32
BF16 = jnp.bfloat16


PLACES = ((3, 2, 1, 0), (3, 2, 0, 1), (0, 1, 3, 2), (0, 1, 2, 3))


def nn(left, right):
    return lax.dot_general(left, right, (((1,), (0,)), ((), ())), preferred_element_type=F32)


def nt(left, right):
    return lax.dot_general(left, right, (((1,), (1,)), ((), ())), preferred_element_type=F32)


def tn(left, right):
    return lax.dot_general(left, right, (((0,), (0,)), ((), ())), preferred_element_type=F32)


def tiles(count):
    size = count // 2 if count % 32 == 0 else count
    return [slice(i * size, (i + 1) * size) for i in range(count // size)]


def column_kernel(near, levels, carried, place_ref, *refs):
    slots = near + levels
    rows, refs = refs[:slots], refs[slots:]
    w_ref, lr_ref, right_ref, grad_ref, *refs = refs
    if carried:
        refs = refs[2:]
    act_ref, back_ref, keep_ref, give_ref, split_ref = refs
    for tile in tiles(act_ref.shape[0]):
        pre = nn(lr_ref[tile, :], right_ref[...])
        for slot in range(slots):
            pre += nn(rows[slot][tile, :], w_ref[0, slot])
        sig = jax.nn.sigmoid(pre)
        act_ref[tile, :] = (pre * sig).astype(BF16)
        back = grad_ref[tile, :].astype(F32) * sig * (1.0 + pre * (1.0 - sig))
        back_ref[tile, :] = back.astype(BF16)
    back = back_ref[...]
    for slot in range(slots + 1):
        left = lr_ref[...] if slot == slots else rows[slot][...]
        split_ref[slot] = tn(left, back).astype(BF16).reshape(split_ref.shape[1:])
    core = place_ref[0]
    for order in range(keep_ref.shape[0]):
        chip = place_ref[1 + order]
        for slot in range(slots + 1):
            keep_ref[order, 0, slot] = split_ref[slot, chip, core]
            give_ref[order, 0, slot] = split_ref[slot, chip, 1 - core]


def row_kernel(near, levels, carried, *refs):
    backs, refs = refs[:near], refs[near:]
    w_near, refs = refs[:near], refs[near:]
    w_far, refs = refs[:levels], refs[levels:]
    right_ref, *refs = refs
    if carried:
        before_ref, refs = refs[0], refs[2 + levels :]
    own_ref, *refs = refs
    far_refs, refs = refs[:levels], refs[levels:]
    low_ref, own_sum, far_sum = refs
    row, col = pl.program_id(0), pl.program_id(1)
    last = col == pl.num_programs(1) - 1

    @pl.when(col == 0)
    def _():
        own_sum[...] = jnp.zeros_like(own_sum)
        far_sum[...] = jnp.zeros_like(far_sum)

    @pl.when(jnp.logical_and(row == 0, col == 0))
    def _():
        low_ref[...] = before_ref[...] if carried else jnp.zeros_like(low_ref)

    for tile in tiles(own_ref.shape[0]):
        total = own_sum[tile, :]
        for slot in range(near):
            total += nt(backs[slot][tile, :], w_near[slot][0, 0])
        own_sum[tile, :] = total
        home = backs[0][tile, :]
        for level in range(levels):
            far_sum[level, tile, :] += nt(home, w_far[level][0, 0])
        low_ref[tile, :] += nt(home, right_ref[...])

    @pl.when(last)
    def _():
        own_ref[...] = own_sum[...].astype(BF16)
        for level in range(levels):
            far_refs[level][...] = far_sum[level].astype(BF16)


def pick(parts, table, place):
    return lax.dynamic_index_in_dim(parts, jnp.asarray(table, jnp.int32)[place], 0, False)


def line_scatter(keep, give, tok_count):
    chips = tok_count // 2
    place = lax.axis_index("tok") // 2

    def move(value, pairs):
        return lax.ppermute(value, "tok", pairs)

    got = move(give, [(i, i ^ 1) for i in range(tok_count)])

    def both(pairs):
        return [(a * 2 + c, b * 2 + c) for a, b in pairs for c in range(2)]

    if chips == 4:

        def term(orders, *more):
            values, wanted = [value for value, _ in more], [index for _, index in more]
            own, other, *values = lax.optimization_barrier((keep, got, *values))
            total = own[orders].astype(F32) + other[orders].astype(F32)
            for value, index in zip(values, wanted):
                total += value[index].astype(F32)
            return total.astype(BF16)

        outer = both([(0, 1), (1, 0), (2, 3), (3, 2)])
        inner = both([(1, 2), (2, 1)])
        pair = move(term(slice(0, 2)), outer)
        passed = move(term(slice(0, 2), (pair, slice(None))), inner)
        third = move(term(2, (passed, 0)), outer)
        return term(3, (third, slice(None)), (passed, 1))

    def mine(table, *more):
        total = pick(keep, table, place).astype(F32) + pick(got, table, place).astype(F32)
        for value in more:
            total += value.astype(F32)
        return total.astype(BF16)

    up = both([(i, i + 1) for i in range(chips - 1)])
    down = both([(i + 1, i) for i in range(chips - 1)])
    above, below = (), ()
    for step in range(1, chips):
        table = [min(chips - step + i, chips - 1) for i in range(chips)]
        above = (move(mine(table, *above), up),)
        table = [max(step + i - chips, 0) for i in range(chips)]
        below = (move(mine(table, *below), down),)
    return mine(list(range(chips)), *above, *below)


def per_device(tokens, sparse_weight, low_left, low_right, act_grad):
    tok_rows, feat_dev = tokens.shape
    cols_dev, slots, block, _ = sparse_weight.shape
    rank = low_left.shape[1]
    tok_count, hid_count = lax.axis_size("tok"), lax.axis_size("hid")
    local_rows = feat_dev // block
    group = cols_dev // local_rows
    levels = hid_count.bit_length() - 1
    near = slots - levels
    masks = [0] + [1 << bit for bit in range(near - 1)]
    chips = tok_count // 2
    kept = block // tok_count
    core = lax.axis_index("tok") % 2
    places = PLACES if chips == 4 else (tuple(range(chips)),) * chips
    order = jnp.asarray(places, jnp.int32)[lax.axis_index("tok") // 2]
    place_arr = jnp.concatenate([jnp.reshape(core, (1,)).astype(jnp.int32), order])

    def partner(value, level):
        return lax.ppermute(value, "hid", [(i, i ^ (1 << level)) for i in range(hid_count)])

    def summed(value):
        for level in range(levels):
            value = (value.astype(F32) + partner(value, level).astype(F32)).astype(BF16)
        return value

    if local_rows >= 6 and local_rows % 2 == 0:
        sizes = [1, 1, 1] + [2] * ((local_rows - 4) // 2) + [1]
    else:
        sizes = [1] * local_rows
    starts = [sum(sizes[:i]) for i in range(len(sizes))]

    low_rank = summed(jnp.dot(tokens, low_left, preferred_element_type=F32).astype(BF16))
    pieces = starts[:3] + [local_rows] if len(sizes) > 3 else starts + [local_rows]
    if len(sizes) > 3:
        pieces.insert(3, starts[3])
    far = []
    for g0, g1 in zip(pieces, pieces[1:]):
        piece = tokens[:, g0 * block : g1 * block]
        far.append([partner(piece, level) for level in range(levels)])

    big = jax.ShapeDtypeStruct(act_grad.shape, BF16)
    carry = ()
    finals = []
    for g0, size in zip(starts, sizes):
        count = size * group
        j0 = g0 * group

        def row_of(i, mask, g0=g0):
            return (g0 + i // group) ^ mask

        in_specs = [pl.BlockSpec((tok_rows, block), lambda i, s, m=m, f=row_of: (0, f(i, m))) for m in masks]
        piece = max(i for i in range(len(far)) if pieces[i] <= g0)
        skip = g0 - pieces[piece]
        in_specs += [pl.BlockSpec((tok_rows, block), lambda i, s, skip=skip: (0, skip + i // group))] * levels
        col_spec = pl.BlockSpec((tok_rows, block), lambda i, s, j0=j0: (0, j0 + i))
        in_specs += [
            pl.BlockSpec((1, slots, block, block), lambda i, s, j0=j0: (j0 + i, 0, 0, 0)),
            pl.BlockSpec((tok_rows, rank), lambda i, s: (0, 0)),
            pl.BlockSpec((rank, block), lambda i, s, j0=j0: (0, j0 + i)),
            col_spec,
        ]
        in_specs += [pl.BlockSpec(memory_space=pl.ANY)] * len(carry)
        part_spec = pl.BlockSpec((chips, 1, slots + 1, kept, block), lambda i, s: (0, i, 0, 0, 0))
        part = jax.ShapeDtypeStruct((chips, count, slots + 1, kept, block), BF16)
        base = len(in_specs) - len(carry) + 1
        column_call = pl.pallas_call(
            functools.partial(column_kernel, near, levels, bool(carry)),
            grid_spec=pltpu.PrefetchScalarGridSpec(
                num_scalar_prefetch=1,
                grid=(count,),
                in_specs=in_specs,
                out_specs=[col_spec, col_spec, part_spec, part_spec],
                scratch_shapes=[pltpu.VMEM((slots + 1, chips, 2, kept, block), BF16)],
            ),
            out_shape=[big, big, part, part],
            input_output_aliases={base: 0, base + 1: 1} if carry else {},
            cost_estimate=pl.CostEstimate(
                flops=4 * count * (slots + 1) * tok_rows * block * block,
                bytes_accessed=2 * count * block * (2 * slots * block + 3 * tok_rows + 2 * rank),
                transcendentals=count * tok_rows * block,
            ),
        )
        column_args = (
            place_arr,
            *[tokens] * near,
            *far[piece],
            sparse_weight,
            low_rank,
            low_right,
            act_grad,
            *carry,
        )
        act, back, keep, give = column_call(*column_args)
        carry = (act, back)
        finals.append(line_scatter(keep, give, tok_count))
    activated, back = carry

    feat = jax.ShapeDtypeStruct((tok_rows, feat_dev), BF16)
    low_spec = pl.BlockSpec((tok_rows, rank), lambda r, c: (0, 0))
    span = max(local_rows // 4, 1)
    parts = ()
    for r0 in range(0, local_rows, span):

        def col_of(r, c, mask, r0=r0):
            return ((r0 + r) ^ mask) * group + c

        in_specs = [pl.BlockSpec((tok_rows, block), lambda r, c, m=m, f=col_of: (0, f(r, c, m))) for m in masks]
        in_specs += [
            pl.BlockSpec((1, 1, block, block), lambda r, c, k=k, m=m, f=col_of: (f(r, c, m), k, 0, 0))
            for k, m in enumerate(masks + [0] * levels)
        ]
        in_specs += [pl.BlockSpec((rank, block), lambda r, c, f=col_of: (0, f(r, c, 0)))]
        base = len(in_specs)
        if parts:
            in_specs += [low_spec] + [pl.BlockSpec(memory_space=pl.ANY)] * (1 + levels)
        feat_spec = pl.BlockSpec((tok_rows, block), lambda r, c, r0=r0: (0, r0 + r))
        row_call = pl.pallas_call(
            functools.partial(row_kernel, near, levels, bool(parts)),
            grid=(span, group),
            in_specs=in_specs,
            out_specs=[feat_spec] * (1 + levels) + [low_spec],
            out_shape=[feat] * (1 + levels) + [jax.ShapeDtypeStruct((tok_rows, rank), F32)],
            scratch_shapes=[
                pltpu.VMEM((tok_rows, block), F32),
                pltpu.VMEM((levels, tok_rows, block), F32),
            ],
            input_output_aliases={base + 1 + i: i for i in range(1 + levels)} if parts else {},
            cost_estimate=pl.CostEstimate(
                flops=2 * span * group * (slots + 1) * tok_rows * block * block,
                bytes_accessed=2 * span * group * block * (slots * block + near * tok_rows + rank),
                transcendentals=0,
            ),
        )
        *parts, low_part = row_call(*[back] * near, *[sparse_weight] * slots, low_right, *parts)
        parts = (low_part, *parts)
    low_part, own_part, *sent = parts
    low_back = summed(low_part.astype(BF16))
    row_sum = own_part.astype(F32)
    for level in range(levels):
        row_sum += partner(sent[level], level).astype(F32)
    tok_grad = (row_sum + nt(low_back, low_left)).astype(BF16)

    left_t = nn(low_back.T, tokens).astype(BF16).reshape(chips, 2, rank // tok_count, feat_dev)
    left_t = jnp.take(left_t, order, axis=0, unique_indices=True, mode="clip")
    left = line_scatter(
        lax.dynamic_index_in_dim(left_t, core, 1, False),
        lax.dynamic_index_in_dim(left_t, 1 - core, 1, False),
        tok_count,
    )
    weight_grad = jnp.concatenate([part[:, :slots] for part in finals], axis=0)
    right_grad = jnp.concatenate(
        [part[:, slots].transpose(1, 0, 2).reshape(kept, -1) for part in finals], axis=1
    )
    return activated, tok_grad, weight_grad, left.T, right_grad


def solution(mesh):
    in_specs = (
        P("tok", "hid"),
        P("hid", None, None, None),
        P("hid", None),
        P(None, "hid"),
        P("tok", "hid"),
    )
    out_specs = (
        P("tok", "hid"),
        P("tok", "hid"),
        P("hid", None, "tok", None),
        P("hid", "tok"),
        P("tok", "hid"),
    )

    return jax.shard_map(
        per_device, mesh=mesh, in_specs=in_specs, out_specs=out_specs, check_vma=False
    )
```
